32 devices in a mesh: sub: 16 (over z, y, x), grp: 2 (over core).
Axes of the slice: x: 2, y: 2, z: 4, core: 2. Of those that a mesh axis runs over, the one named last changes fastest.
Arguments:
- interior_factor: bfloat16 [16, 1024, 1024], P('sub'), may hold values from -2 to 2, as said below
- coupling: bfloat16 [16, 512, 1024], P('sub', 'grp'), may hold values from -0.09375 to 0.09375
- boundary_stiffness: float32 [16, 512, 512], P('sub', 'grp'), may hold values from -0.65625 to 9, as said below
- interior_mass: float32 [16, 1024], P('sub'), may hold values from 0.5 to 4
- boundary_mass: float32 [16, 512], P('sub', 'grp'), may hold values from 0.5 to 2
- dof_map: int32 [16, 256], P('sub'), may hold values from 0 to 255, each once within a row
- load_cases: float32 [16, 64, 256], P('sub'), may hold values from -30 to 30
Outputs:
- reduced_stiffness: float32 [16, 256, 256], P('sub')
- reduced_mass: float32 [16, 256, 256], P('sub')
- displacement: float32 [16, 64, 256], P('sub')
The draws below stay inside these ranges and needn't reach their ends.
Inputs may be any that keep to these rules, and one draw needn't show every extreme that they name: `interior_factor`: lower triangular; diagonal between 1 and 2. `boundary_stiffness`: symmetric; diagonal between 6 and 9. `dof_map`: each row a permutation of 0 to 255.
All inputs are finite; a program needn't handle non-finite values.
Results may differ from the reference program's by a relative error of at most 0.00095.
Values may be sent and summed in bfloat16 or wider, within the bound.
A program may use at most 64 MiB of HBM per device.

```python
import math
import jax
import jax.numpy as jnp
from jax import lax

NI = 1024
NB = 512
NRHS = 64
ITERS = 2
FACE = 256
NS = 16


def draw_interior_factor(key, part):
    first_key, second_key = jax.random.split(jax.random.fold_in(key, 11))
    lower_part = jnp.clip(jax.random.normal(first_key, (NS, NI, NI), jnp.float32), -4.0, 4.0) * (1.0 / NI ** 0.5)
    diagonal = jax.random.uniform(second_key, (NS, NI), jnp.float32, 1.0, 2.0)
    lower_part = jnp.tril(lower_part, -1)
    result = lower_part + jnp.eye(NI, dtype=jnp.float32)[None] * diagonal[:, None, :]
    return result.astype(jnp.bfloat16)


def draw_coupling(key, part):
    first_key = jax.random.fold_in(jax.random.fold_in(key, 37), 0)
    entries = jnp.clip(jax.random.normal(first_key, (NS, NB, NI), jnp.float32), -4.0, 4.0)
    result = entries * (0.5 / NI ** 0.5)
    return result.astype(jnp.bfloat16)


def draw_boundary_stiffness(key, part):
    first_key, second_key = jax.random.split(jax.random.fold_in(key, 23))
    raw = jnp.clip(jax.random.normal(first_key, (NS, NB, NB), jnp.float32), -4.0, 4.0)
    diagonal = jax.random.uniform(second_key, (NS, NB), jnp.float32, 6.0, 9.0)
    symmetric = (raw + jnp.swapaxes(raw, 1, 2)) / (2.0 * NB) ** 0.5
    row_face = lax_rows = jnp.arange(NB, dtype=jnp.int32)[:, None] < NB // 2
    col_face = jnp.arange(NB, dtype=jnp.int32)[None, :] < NB // 2
    same_face = row_face == col_face
    profile = jnp.where(same_face, 0.3, 2.6).astype(jnp.float32)
    eye_mask = jnp.eye(NB, dtype=jnp.float32)[None]
    return symmetric * profile[None] * (1.0 - eye_mask) + eye_mask * diagonal[:, None, :]


def block_levels(own_key, dims, cuts, smallest, largest):
    def one(axis_at, shards_of):
        steps = jax.random.uniform(jax.random.fold_in(jax.random.fold_in(own_key, 6), axis_at), (shards_of,), jnp.float32, smallest / len(cuts), largest / len(cuts))
        return jnp.repeat(jnp.exp(steps), dims[axis_at] // shards_of).reshape((-1,) + (1,) * (len(dims) - axis_at - 1))

    factor_of = one(*cuts[0])
    for cut in cuts[1:]:
        factor_of = factor_of * one(*cut)
    return factor_of


def normal_values(stream_key, shape, spread, bound, cuts=(), held_as=jnp.bfloat16):
    drawn = spread * jax.random.normal(stream_key, shape, jnp.float32)
    if cuts:
        drawn = drawn * block_levels(stream_key, shape, cuts, -0.22, 0.18)
    return jnp.clip(drawn, -bound, bound).astype(held_as)


def setup_inputs(seed: int = 0) -> dict:
    key_list = jax.random.split(jax.random.key(seed), 8)
    return {
        "interior_factor": draw_interior_factor(jax.random.fold_in(key_list[7], 71), 0),
        "coupling": draw_coupling(jax.random.fold_in(key_list[7], 71), 0),
        "boundary_stiffness": draw_boundary_stiffness(jax.random.fold_in(key_list[7], 71), 0),
        "interior_mass": jnp.clip(jnp.exp(math.log(4.0) - 2.0794415 * jax.random.uniform(key_list[3], (NS, NI), jnp.float32) ** block_levels(key_list[3], (NS, NI), ((0, 16),), -0.2, 0.2)), 0.5, 4.0),
        "boundary_mass": jnp.clip(jnp.exp(math.log(2.0) - 1.3862944 * jax.random.uniform(key_list[4], (NS, NB), jnp.float32) ** block_levels(key_list[4], (NS, NB), ((0, 16), (1, 2)), -0.2, 0.2)), 0.5, 2.0),
        "dof_map": jax.vmap(lambda own: jax.random.permutation(own, FACE))(jax.random.split(key_list[5], NS)).reshape((NS, FACE)).astype(jnp.int32),
        "load_cases": normal_values(key_list[6], (NS, NRHS, FACE), 5.0, 30.0, ((0, 16),), jnp.float32),
    }


HIGH = lax.Precision.HIGHEST

def reduce_single(items):
    factor_low, coupling_rows, stiff, weights, bound_mass = items
    factor = factor_low.astype(jnp.float32)
    modes_w = jax.scipy.linalg.solve_triangular(factor, coupling_rows.astype(jnp.float32).T, lower=True)
    constraint = -jax.scipy.linalg.solve_triangular(factor, modes_w, lower=True, trans=1)
    schur = stiff - jnp.dot(modes_w.T, modes_w, precision=HIGH)
    mass_red = jnp.diag(bound_mass) + jnp.dot(constraint.T, weights[:, None] * constraint, precision=HIGH)
    return (schur, mass_red)

def invert_map(mapping):
    count = mapping.shape[0]
    return jnp.zeros((count,), jnp.int32).at[mapping].set(jnp.arange(count, dtype=jnp.int32))

def reference(interior_factor, coupling, boundary_stiffness, interior_mass, boundary_mass, dof_map, load_cases):
    schur_all, mass_all = lax.map(reduce_single, (interior_factor, coupling, boundary_stiffness, interior_mass, boundary_mass))
    half = FACE
    inverse = jax.vmap(invert_map)(dof_map)
    permute = jax.vmap(lambda block, order: block[order][:, order])
    shared_stiff = permute(schur_all[:, half:, half:], inverse)
    shared_mass = permute(mass_all[:, half:, half:], inverse)
    reduced_stiffness = schur_all[:, :half, :half] + jnp.roll(shared_stiff, -1, axis=0)
    reduced_mass = mass_all[:, :half, :half] + jnp.roll(shared_mass, -1, axis=0)
    factors = jax.vmap(jnp.linalg.cholesky)(reduced_stiffness)

    def precondition(values):
        return jax.vmap(lambda low, rows: jax.scipy.linalg.cho_solve((low, True), rows.T).T)(factors, values)

    def operate(values):
        previous = jnp.roll(values, 1, axis=0)
        taken = jax.vmap(lambda rows, order: jnp.take(rows, order, axis=1))(previous, dof_map)
        local_dirs = jnp.concatenate([values, taken], axis=2)
        images = jnp.einsum('snb,scb->snc', local_dirs, schur_all, precision=HIGH)
        owned = images[:, :, :half]
        shared = jax.vmap(lambda rows, order: jnp.take(rows, order, axis=1))(images[:, :, half:], inverse)
        return owned + jnp.roll(shared, -1, axis=0)

    def inner_sum(left, right):
        return jnp.einsum('snf,smf->nm', left, right, precision=HIGH)

    def chol_solve(matrix, right):
        return jax.scipy.linalg.cho_solve((jnp.linalg.cholesky(matrix), True), right)
    solution = jnp.zeros_like(load_cases)
    residual = load_cases
    smoothed = precondition(residual)
    rho_sum = inner_sum(residual, smoothed)
    direction = smoothed
    for step in range(ITERS):
        images = operate(direction)
        gamma_sum = inner_sum(direction, images)
        step_coeffs = chol_solve(gamma_sum, rho_sum)
        solution = solution + jnp.einsum('mn,smf->snf', step_coeffs, direction, precision=HIGH)
        residual = residual - jnp.einsum('mn,smf->snf', step_coeffs, images, precision=HIGH)
        if step + 1 < ITERS:
            smoothed = precondition(residual)
            rho_next = inner_sum(residual, smoothed)
            next_coeffs = chol_solve(rho_sum, rho_next)
            direction = smoothed + jnp.einsum('mn,smf->snf', next_coeffs, direction, precision=HIGH)
            rho_sum = rho_next
    return (reduced_stiffness, reduced_mass, solution)
```

```python
import functools
import jax
import jax.numpy as jnp
from jax import lax
from jax.experimental import pallas as pl
from jax.experimental.pallas import tpu as pltpu
from jax.sharding import PartitionSpec as P

F32 = jnp.float32
BF16 = jnp.bfloat16
HIGH = lax.Precision.HIGHEST
TILE = 128
VMEM_LIMIT = 48 * 2**20
NT = (((1,), (1,)), ((), ()))
NN = (((1,), (0,)), ((), ()))
TN = (((0,), (0,)), ((), ()))


def dot(a, b, dims=NN):
    return lax.dot_general(a, b, dims, preferred_element_type=F32)


def fdot(a, b, dims=NN):
    return lax.dot_general(a, b, dims, precision=HIGH, preferred_element_type=F32)


def split(x):
    hi = x.astype(BF16)
    return hi, (x - hi.astype(F32)).astype(BF16)


def dot3(a, b, dims=NN):
    ah, al = split(a)
    bh, bl = split(b)
    return dot(ah, bh, dims) + (dot(ah, bl, dims) + dot(al, bh, dims))


def iota(shape, dim):
    return lax.broadcasted_iota(jnp.int32, shape, dim)


def modes_kernel(l_ref, c_ref, w_ref, k_ref, inv, wh, wl):
    ni = l_ref.shape[0]
    count = ni // TILE
    rows = iota((TILE, TILE), 0)
    cols = iota((TILE, TILE), 1)

    def block(j):
        return l_ref[j * TILE : (j + 1) * TILE, j * TILE : (j + 1) * TILE]

    pair = ((rows >> 1) == (cols >> 1)) & (rows > cols)
    for j in range(count):
        full = block(j).astype(F32)
        diag = jnp.where(rows == cols, full, 0.0)
        down = 1.0 / jnp.sum(diag, axis=1, keepdims=True)
        across = 1.0 / jnp.sum(diag, axis=0, keepdims=True)
        first = jnp.where(rows == cols, down, 0.0)
        inv[j] = first - jnp.where(pair, down * full * across, 0.0)

    levels = TILE.bit_length() - 1

    def level(lev, carry):
        same = (rows >> (lev + 1)) == (cols >> (lev + 1))
        low = ((rows >> lev) & 1) > ((cols >> lev) & 1)
        mask = same & low
        for j in range(count):
            x = inv[j]
            off = jnp.where(mask, block(j).astype(F32), 0.0).astype(BF16)
            xh, xl = split(x)
            mid = dot(xh, off) + dot(xl, off)
            mh, ml = split(mid)
            inv[j] = x - (dot(mh, xh) + (dot(mh, xl) + dot(ml, xh)))
        return carry

    lax.fori_loop(1, levels, level, 0)

    for j in range(count):
        at = slice(j * TILE, (j + 1) * TILE)
        acc = c_ref[:, at].astype(F32)
        if j:
            before = slice(0, j * TILE)
            acc = acc - (
                dot(wh[:, before], l_ref[at, before], NT)
                + dot(wl[:, before], l_ref[at, before], NT)
            )
        piece = dot3(acc, inv[j], NT)
        hi, lo = split(piece)
        wh[:, at] = hi
        wl[:, at] = lo
        w_ref[:, at] = hi
    for j in reversed(range(count)):
        at = slice(j * TILE, (j + 1) * TILE)
        acc = wh[:, at].astype(F32) + wl[:, at].astype(F32)
        if j + 1 < count:
            after = slice((j + 1) * TILE, ni)
            acc = acc + (dot(wh[:, after], l_ref[after, at]) + dot(wl[:, after], l_ref[after, at]))
        piece = -dot3(acc, inv[j])
        hi, lo = split(piece)
        wh[:, at] = hi
        wl[:, at] = lo
        k_ref[:, at] = hi


def modes(factor, coupling):
    width, ni = coupling.shape
    return pl.pallas_call(
        modes_kernel,
        out_shape=[jax.ShapeDtypeStruct((width, ni), BF16)] * 2,
        scratch_shapes=[
            pltpu.VMEM((ni // TILE, TILE, TILE), F32),
            pltpu.VMEM((width, ni), BF16),
            pltpu.VMEM((width, ni), BF16),
        ],
        compiler_params=pltpu.CompilerParams(vmem_limit_bytes=VMEM_LIMIT),
        name="modes",
    )(factor, coupling)


def faces_kernel(w_ref, k_ref, stiff_ref, mass_ref, bound_ref, map_ref, own_ref, move_ref, om_ref, mm_ref):
    half = stiff_ref.shape[0] // 2
    wo, ws = w_ref[:half], w_ref[half:]
    own_ref[...] = stiff_ref[:half, :half] - dot(wo, wo, NT)
    shared = stiff_ref[half:, half:] - dot(ws, ws, NT)
    cross = stiff_ref[half:, :half] - dot(ws, wo, NT)
    weights = mass_ref[...]
    eye = iota((half, half), 0) == iota((half, half), 1)

    def mass_of(c, b):
        ch, cl = split(c.astype(F32) * weights)
        return dot(ch, c, NT) + dot(cl, c, NT) + jnp.where(eye, b, 0.0)

    om_ref[...] = mass_of(k_ref[:half], bound_ref[:, :half])
    mass_shared = mass_of(k_ref[half:], bound_ref[:, half:])
    q = jnp.where(iota((half, half), 0) == map_ref[...], 1.0, 0.0).astype(F32)
    move_ref[0] = fdot(fdot(q, shared), q, NT)
    move_ref[1] = fdot(q, cross)
    mm_ref[...] = fdot(fdot(q, mass_shared), q, NT)


def faces(w, k, stiff, mass, bound, mapping):
    half = stiff.shape[0] // 2
    block = jax.ShapeDtypeStruct((half, half), F32)
    return pl.pallas_call(
        faces_kernel,
        out_shape=[block, jax.ShapeDtypeStruct((2, half, half), F32), block, block],
        compiler_params=pltpu.CompilerParams(vmem_limit_bytes=VMEM_LIMIT),
        name="faces",
    )(w, k, stiff, mass, bound, mapping)


def sweep(a, size):
    width = a.shape[1]
    lane = iota(a.shape, 1)
    row_at = iota(a.shape, 0)
    groups = width // size
    for k in range(size):
        col = a[:, k : k + 1]
        pivot = a[k : k + 1, k : k + 1]
        here = lane == k
        if groups == 1:
            col = jnp.broadcast_to(col, a.shape)
            pivot = jnp.broadcast_to(pivot, (1, width))
        else:
            col = jnp.where(lane < size, col, a[:, size + k : size + k + 1])
            pivot = jnp.where(lane[:1] < size, pivot, a[k : k + 1, size + k : size + k + 1])
            here = (lane == k) | (lane == size + k)
        scale = 1.0 / pivot
        row = jnp.where(here[:1], scale, a[k : k + 1, :] * scale)
        a = jnp.where(row_at == k, row, jnp.where(here, 0.0, a) - col * row)
    return a


def invert(ref, step):
    n = ref.shape[0]
    for p in range(n // step):
        at = slice(p * step, (p + 1) * step)
        pin = sweep(ref[at, at], step)
        panel = ref[at, :]
        col = ref[:, at]
        inside = (iota((step, n), 1) // step) == p
        row = jnp.where(inside, 0.0, fdot(pin, panel))
        left = (iota((n, step), 0) // step) == p
        colz = jnp.where(left, 0.0, col)
        ref[...] = ref[...] - fdot(colz, row)
        ref[:, at] = -fdot(colz, pin)
        ref[at, :] = row
        ref[at, at] = pin


STEP = 64


def begin_kernel(own_ref, move_ref, loads_ref, red_ref, inv_ref, z_ref, work):
    reduced = own_ref[...] + move_ref[0]
    red_ref[...] = reduced
    work[...] = reduced
    invert(work, STEP)
    inv_ref[...] = work[...]
    z_ref[...] = fdot(loads_ref[...], work[...])


def begin(own, moved, loads):
    half = own.shape[0]
    block = jax.ShapeDtypeStruct((half, half), F32)
    return pl.pallas_call(
        begin_kernel,
        out_shape=[block, block, jax.ShapeDtypeStruct(loads.shape, F32)],
        scratch_shapes=[pltpu.VMEM((half, half), F32)],
        compiler_params=pltpu.CompilerParams(vmem_limit_bytes=VMEM_LIMIT),
        name="begin",
    )(own, moved, loads)


def finish_kernel(g_ref, z_ref, sy_ref, out_ref):
    n = z_ref.shape[0]
    rho, gamma, kappa, delta = (g_ref[i] for i in range(4))
    both = sweep(jnp.concatenate([gamma, rho], axis=1), n)
    gamma_inv, rho_inv = both[:, :n], both[:, n:]
    c1 = fdot(gamma_inv, rho)
    cross = fdot(gamma, c1)
    rho_next = rho - cross - cross.T + fdot(c1, fdot(kappa, c1), TN)
    beta = fdot(rho_inv, rho_next)
    eye = jnp.where(iota((n, n), 0) == iota((n, n), 1), 1.0, 0.0)
    pb = eye + beta
    mixed = fdot(pb, fdot(kappa, c1), TN)
    gamma2 = fdot(pb, fdot(gamma, pb), TN) - mixed - mixed.T + fdot(c1, fdot(delta, c1), TN)
    c2 = fdot(sweep(gamma2, n), rho_next)
    out_ref[...] = fdot(c1 + fdot(pb, c2), z_ref[...], TN) - fdot(fdot(c1, c2), sy_ref[...], TN)


def finish(grams, z, sy):
    return pl.pallas_call(
        finish_kernel,
        out_shape=jax.ShapeDtypeStruct(z.shape, F32),
        compiler_params=pltpu.CompilerParams(vmem_limit_bytes=VMEM_LIMIT),
        name="finish",
    )(grams, z, sy)


def passed_along(array, axis, by):
    size = lax.axis_size(axis)
    return lax.ppermute(array, axis, [(i, (i + by) % size) for i in range(size)])


def summed(array, axis):
    size = lax.axis_size(axis)
    bit = 1
    while bit < size:
        array = array + lax.ppermute(array, axis, [(i, i ^ bit) for i in range(size)])
        bit *= 2
    return array


def shards(
    interior_factor, coupling, boundary_stiffness, interior_mass, boundary_mass, dof_map, load_cases
):
    w_own, k_own = modes(interior_factor[0], coupling[0])
    stiff = lax.all_gather(boundary_stiffness[0], "grp", axis=0, tiled=True)
    bound = lax.all_gather(boundary_mass[0], "grp", axis=0, tiled=True)
    w = lax.all_gather(w_own, "grp", axis=0, tiled=True)
    k = lax.all_gather(k_own, "grp", axis=0, tiled=True)
    own, move, own_mass, move_mass = faces(
        w, k, stiff, interior_mass, bound[None], dof_map
    )
    moved = passed_along(move, "sub", -1)
    moved_mass = passed_along(move_mass, "sub", -1)
    loads = load_cases[0]
    reduced, inverse, z = begin(own, moved, loads)

    def operate(v):
        return (
            fdot(v, reduced)
            + fdot(passed_along(v, "sub", 1), move[1])
            + fdot(passed_along(v, "sub", -1), moved[1], NT)
        )

    y = operate(z)
    sy = fdot(y, inverse)
    y2 = operate(sy)
    grams = summed(
        jnp.stack([fdot(loads, z, NT), fdot(z, y, NT), fdot(y, sy, NT), fdot(sy, y2, NT)]), "sub"
    )
    return (reduced[None], (own_mass + moved_mass)[None], finish(grams, z, sy)[None])


def solution(mesh):
    return jax.shard_map(
        shards,
        mesh=mesh,
        in_specs=(
            P("sub", None, None),
            P("sub", "grp", None),
            P("sub", "grp", None),
            P("sub", None),
            P("sub", "grp"),
            P("sub", None),
            P("sub", None, None),
        ),
        out_specs=(P("sub", None, None), P("sub", None, None), P("sub", None, None)),
        check_vma=False,
    )
```

```python
import functools
import jax
import jax.numpy as jnp
from jax import lax
from jax.experimental import pallas as pl
from jax.experimental.pallas import tpu as pltpu
from jax.sharding import PartitionSpec as P

F32 = jnp.float32
BF16 = jnp.bfloat16
HIGH = lax.Precision.HIGHEST
TILE = 128
VMEM_LIMIT = 48 * 2**20
NT = (((1,), (1,)), ((), ()))
NN = (((1,), (0,)), ((), ()))
TN = (((0,), (0,)), ((), ()))


def dot(a, b, dims=NN):
    return lax.dot_general(a, b, dims, preferred_element_type=F32)


def fdot(a, b, dims=NN):
    return lax.dot_general(a, b, dims, precision=HIGH, preferred_element_type=F32)


def split(x):
    hi = x.astype(BF16)
    return hi, (x - hi.astype(F32)).astype(BF16)


def dot3(a, b, dims=NN):
    ah, al = split(a)
    bh, bl = split(b)
    return dot(ah, bh, dims) + (dot(ah, bl, dims) + dot(al, bh, dims))


def iota(shape, dim):
    return lax.broadcasted_iota(jnp.int32, shape, dim)


def solve_modes(l_ref, c_ref, put, inv, wh, wl):
    ni = l_ref.shape[0]
    count = ni // TILE
    rows = iota((TILE, TILE), 0)
    cols = iota((TILE, TILE), 1)

    def block(j):
        return l_ref[j * TILE : (j + 1) * TILE, j * TILE : (j + 1) * TILE]

    pair = ((rows >> 1) == (cols >> 1)) & (rows > cols)
    for j in range(count):
        full = block(j).astype(F32)
        diag = jnp.where(rows == cols, full, 0.0)
        down = 1.0 / jnp.sum(diag, axis=1, keepdims=True)
        across = 1.0 / jnp.sum(diag, axis=0, keepdims=True)
        first = jnp.where(rows == cols, down, 0.0)
        inv[j] = first - jnp.where(pair, down * full * across, 0.0)

    levels = TILE.bit_length() - 1

    def level(lev, carry):
        same = (rows >> (lev + 1)) == (cols >> (lev + 1))
        low = ((rows >> lev) & 1) > ((cols >> lev) & 1)
        mask = same & low
        for j in range(count):
            x = inv[j]
            off = jnp.where(mask, block(j).astype(F32), 0.0).astype(BF16)
            xh, xl = split(x)
            mid = dot(xh, off) + dot(xl, off)
            mh, ml = split(mid)
            inv[j] = x - (dot(mh, xh) + (dot(mh, xl) + dot(ml, xh)))
        return carry

    lax.fori_loop(1, levels, level, 0)

    for j in range(count):
        at = slice(j * TILE, (j + 1) * TILE)
        acc = c_ref[:, at].astype(F32)
        if j:
            before = slice(0, j * TILE)
            acc = acc - (
                dot(wh[:, before], l_ref[at, before], NT)
                + dot(wl[:, before], l_ref[at, before], NT)
            )
        piece = dot3(acc, inv[j], NT)
        hi, lo = split(piece)
        wh[:, at] = hi
        wl[:, at] = lo
    put(0)
    for j in reversed(range(count)):
        at = slice(j * TILE, (j + 1) * TILE)
        acc = wh[:, at].astype(F32) + wl[:, at].astype(F32)
        if j + 1 < count:
            after = slice((j + 1) * TILE, ni)
            acc = acc + (dot(wh[:, after], l_ref[after, at]) + dot(wl[:, after], l_ref[after, at]))
        piece = -dot3(acc, inv[j])
        hi, lo = split(piece)
        wh[:, at] = hi
        wl[:, at] = lo
    put(1)


def at_device(sub, grp):
    return dict(device_id=(sub, grp), device_id_type=pl.DeviceIdType.MESH)


def substructure_kernel(
    l_ref, c_ref, rows_ref, mass_ref, bound_ref, map_ref,
    own_ref, move_ref, om_ref, mm_ref,
    inv, wh, wl, both, stiff, bound, send, recv,
):
    grp = lax.axis_index("grp")
    sub = lax.axis_index("sub")
    members = lax.axis_size("grp")
    width = c_ref.shape[0]
    mine = pl.ds(pl.multiple_of(grp * width, width), width)
    others = [lax.rem(grp + d, members) for d in range(1, members)]

    barrier = pltpu.get_barrier_semaphore()
    for other in others:
        pl.semaphore_signal(barrier, inc=1, **at_device(sub, other))
    pl.semaphore_wait(barrier, members - 1)

    copies = []

    def spread(item, src, dst):
        for d, other in enumerate(others):
            copy = pltpu.make_async_remote_copy(
                src_ref=src, dst_ref=dst,
                send_sem=send.at[item, d], recv_sem=recv.at[item, d],
                **at_device(sub, other),
            )
            copy.start()
            copies.append(copy)

    spread(2, rows_ref, stiff.at[mine])
    spread(3, bound_ref, bound.at[grp])
    stiff[mine, :] = rows_ref[...]
    bound[grp] = bound_ref[...]

    def put(item):
        both[item, mine, :] = wh[...]
        spread(item, both.at[item, mine], both.at[item, mine])

    solve_modes(l_ref, c_ref, put, inv, wh, wl)
    for copy in copies:
        copy.wait()

    half = rows_ref.shape[1] // 2
    wo, ws = both[0, :half], both[0, half:]
    own_ref[...] = stiff[:half, :half] - dot(wo, wo, NT)
    shared = stiff[half:, half:] - dot(ws, ws, NT)
    cross = stiff[half:, :half] - dot(ws, wo, NT)
    weights = mass_ref[...]
    eye = iota((half, half), 0) == iota((half, half), 1)
    pieces = jnp.concatenate([bound[i] for i in range(members)], axis=1)

    def mass_of(c, b):
        ch, cl = split(c.astype(F32) * weights)
        return dot(ch, c, NT) + dot(cl, c, NT) + jnp.where(eye, b, 0.0)

    om_ref[...] = mass_of(both[1, :half], pieces[:, :half])
    mass_shared = mass_of(both[1, half:], pieces[:, half:])
    q = jnp.where(iota((half, half), 0) == map_ref[...], 1.0, 0.0).astype(F32)
    move_ref[0] = fdot(fdot(q, shared), q, NT)
    move_ref[1] = fdot(q, cross)
    mm_ref[...] = fdot(fdot(q, mass_shared), q, NT)


def substructure(factor, coupling, rows, mass, bound, mapping):
    width, ni = coupling.shape
    nbound = rows.shape[1]
    half = nbound // 2
    members = nbound // width
    block = jax.ShapeDtypeStruct((half, half), F32)
    peers = max(members - 1, 1)
    return pl.pallas_call(
        substructure_kernel,
        out_shape=[block, jax.ShapeDtypeStruct((2, half, half), F32), block, block],
        in_specs=[pl.BlockSpec(memory_space=pltpu.VMEM)] * 6,
        out_specs=[pl.BlockSpec(memory_space=pltpu.VMEM)] * 4,
        scratch_shapes=[
            pltpu.VMEM((ni // TILE, TILE, TILE), F32),
            pltpu.VMEM((width, ni), BF16),
            pltpu.VMEM((width, ni), BF16),
            pltpu.VMEM((2, nbound, ni), BF16),
            pltpu.VMEM((nbound, nbound), F32),
            pltpu.VMEM((members, 1, width), F32),
            pltpu.SemaphoreType.DMA((4, peers)),
            pltpu.SemaphoreType.DMA((4, peers)),
        ],
        compiler_params=pltpu.CompilerParams(
            vmem_limit_bytes=VMEM_LIMIT, collective_id=0, has_side_effects=True
        ),
        name="substructure",
    )(factor, coupling, rows, mass, bound, mapping)


def sweep(a, size):
    width = a.shape[1]
    lane = iota(a.shape, 1)
    lane_row = lane[:1]
    row_at = iota(a.shape, 0)
    first = lane < size

    def lanes(rows, k):
        if width == size:
            return jnp.broadcast_to(rows[:, k : k + 1], rows.shape)
        left = rows[:, k : k + 1]
        right = rows[:, size + k : size + k + 1]
        return jnp.where(first[: rows.shape[0]], left, right)

    local = jnp.where(first, lane, lane - size)
    local_row = local[:1]
    for k in range(0, size, 2):
        c0, c1 = lanes(a, k), lanes(a, k + 1)
        r0, r1 = a[k : k + 1, :], a[k + 1 : k + 2, :]
        p, q, s = c0[k : k + 1], c1[k : k + 1], c1[k + 1 : k + 2]
        scale = 1.0 / (p * s - q * q)
        ip, iq, ir = s * scale, -q * scale, p * scale
        at0, at1 = local_row == k, local_row == k + 1
        n0 = jnp.where(at0, ip, jnp.where(at1, iq, ip * r0 + iq * r1))
        n1 = jnp.where(at0, iq, jnp.where(at1, ir, iq * r0 + ir * r1))
        inside = (local >> 1) == (k >> 1)
        a = jnp.where(inside, 0.0, a) - c0 * n0 - c1 * n1
        a = jnp.where(row_at == k, n0, jnp.where(row_at == k + 1, n1, a))
    return a


def invert(ref, step):
    n = ref.shape[0]
    for p in range(n // step):
        at = slice(p * step, (p + 1) * step)
        pin = sweep(ref[at, at], step)
        panel = ref[at, :]
        col = ref[:, at]
        inside = (iota((step, n), 1) // step) == p
        row = jnp.where(inside, 0.0, fdot(pin, panel))
        left = (iota((n, step), 0) // step) == p
        colz = jnp.where(left, 0.0, col)
        ref[...] = ref[...] - fdot(colz, row)
        ref[:, at] = -fdot(colz, pin)
        ref[at, :] = row
        ref[at, at] = pin


STEP = 64


def stages_of(size):
    stages, stride = [], 1
    while stride < size:
        radix = 4 if stride * 4 <= size else 2
        stages.append((stride, radix))
        stride *= radix
    return stages


def interface_kernel(
    own_ref, move_ref, om_ref, mm_ref, loads_ref,
    red_ref, mass_ref, out_ref,
    came, came_cross, came_mass, work, z, sy, near, acc, got, total,
    part_send, part_recv, fwd_send, fwd_recv, big_send, big_recv,
    dir_send, dir_recv, sum_send, sum_recv, all_send, all_recv,
):
    grp, sub = lax.axis_index("grp"), lax.axis_index("sub")
    members, size = lax.axis_size("grp"), lax.axis_size("sub")
    ahead, back = lax.rem(sub + 1, size), lax.rem(sub + size - 1, size)
    others = [lax.rem(grp + d, members) for d in range(1, members)]
    half = own_ref.shape[0]
    n = loads_ref.shape[0]
    stages = stages_of(size)

    def partner(stride, radix, d):
        digit = lax.rem(lax.div(sub, stride), radix)
        return sub + (lax.rem(digit + d, radix) - digit) * stride

    barrier = pltpu.get_barrier_semaphore()
    greeted = 0
    for other in others:
        pl.semaphore_signal(barrier, inc=1, **at_device(sub, other))
        greeted += 1
    for to in [ahead, back] + [partner(t, r, d) for t, r in stages for d in range(1, r)]:
        pl.semaphore_signal(barrier, inc=1, **at_device(to, grp))
        greeted += 1
    pl.semaphore_wait(barrier, greeted)

    def remote(src, dst, send, recv, to_sub, to_grp):
        copy = pltpu.make_async_remote_copy(
            src_ref=src, dst_ref=dst, send_sem=send, recv_sem=recv, **at_device(to_sub, to_grp)
        )
        copy.start()
        return copy

    share = half // members
    part = pl.ds(pl.multiple_of(grp * share, share), share)
    first = remote(move_ref.at[0, part], came.at[part], part_send.at[0], part_recv.at[0], back, grp)
    first.wait()
    forwards = [
        remote(came.at[part], came.at[part], fwd_send.at[d], fwd_recv.at[d], sub, other)
        for d, other in enumerate(others)
    ]
    cross_copy = remote(move_ref.at[1], came_cross, big_send.at[0], big_recv.at[0], back, grp)
    for copy in forwards:
        copy.wait()
    mass_copy = remote(mm_ref, came_mass, big_send.at[1], big_recv.at[1], back, grp)

    red_ref[...] = own_ref[...] + came[...]
    work[...] = red_ref[...]
    invert(work, STEP)
    z[...] = fdot(loads_ref[...], work[...])

    def neighbours(v, use):
        return [
            remote(v, near.at[use, 0], dir_send.at[use, 0], dir_recv.at[use, 0], ahead, grp),
            remote(v, near.at[use, 1], dir_send.at[use, 1], dir_recv.at[use, 1], back, grp),
        ]

    def from_neighbours(use):
        return fdot(near[use, 0], move_ref[1]) + fdot(near[use, 1], came_cross[...], NT)

    copies = neighbours(z, 0)
    y = fdot(z[...], red_ref[...])
    rho = fdot(loads_ref[...], z[...], NT)
    cross_copy.wait()
    for copy in copies:
        copy.wait()
    y = y + from_neighbours(0)
    sy[...] = fdot(y, work[...])
    copies = neighbours(sy, 1)
    y2 = fdot(sy[...], red_ref[...])
    gamma = fdot(z[...], y, NT)
    kappa = fdot(y, sy[...], NT)
    acc[0, :n, :n] = rho
    acc[0, :n, n:] = gamma
    acc[0, n:, :n] = kappa
    mass_copy.wait()
    mass_ref[...] = om_ref[...] + came_mass[...]
    for copy in copies:
        copy.wait()
    y2 = y2 + from_neighbours(1)
    acc[0, n:, n:] = fdot(sy[...], y2, NT)

    rows = 2 * n // members
    chunk = pl.ds(pl.multiple_of(grp * rows, rows), rows)
    slot = 0
    for i, (stride, radix) in enumerate(stages):
        copies = [
            remote(
                acc.at[i, chunk], got.at[slot + d - 1],
                sum_send.at[slot + d - 1], sum_recv.at[slot + d - 1],
                partner(stride, radix, d), grp,
            )
            for d in range(1, radix)
        ]
        value = acc[i, chunk, :]
        for d, copy in enumerate(copies):
            copy.wait()
            value = value + got[slot + d]
        acc[i + 1, chunk, :] = value
        slot += radix - 1
    last = len(stages)
    total[chunk, :] = acc[last, chunk, :]
    copies = [
        remote(acc.at[last, chunk], total.at[chunk], all_send.at[d], all_recv.at[d], sub, other)
        for d, other in enumerate(others)
    ]
    for copy in copies:
        copy.wait()

    rho, gamma = total[:n, :n], total[:n, n:]
    kappa, delta = total[n:, :n], total[n:, n:]
    both = sweep(jnp.concatenate([gamma, rho], axis=1), n)
    gamma_inv, rho_inv = both[:, :n], both[:, n:]
    c1 = fdot(gamma_inv, rho)
    cross = fdot(gamma, c1)
    rho_next = rho - cross - cross.T + fdot(c1, fdot(kappa, c1), TN)
    beta = fdot(rho_inv, rho_next)
    eye = jnp.where(iota((n, n), 0) == iota((n, n), 1), 1.0, 0.0)
    pb = eye + beta
    mixed = fdot(pb, fdot(kappa, c1), TN)
    gamma2 = fdot(pb, fdot(gamma, pb), TN) - mixed - mixed.T + fdot(c1, fdot(delta, c1), TN)
    c2 = fdot(sweep(gamma2, n), rho_next)
    out_ref[...] = fdot(c1 + fdot(pb, c2), z[...], TN) - fdot(fdot(c1, c2), sy[...], TN)


def interface(own, move, own_mass, move_mass, loads, size, members):
    half = own.shape[0]
    n = loads.shape[0]
    block = jax.ShapeDtypeStruct((half, half), F32)
    stages = stages_of(size)
    slots = sum(r - 1 for _, r in stages)
    peers = max(members - 1, 1)
    dma = pltpu.SemaphoreType.DMA
    return pl.pallas_call(
        interface_kernel,
        out_shape=[block, block, jax.ShapeDtypeStruct(loads.shape, F32)],
        in_specs=[pl.BlockSpec(memory_space=pltpu.VMEM)] * 5,
        out_specs=[pl.BlockSpec(memory_space=pltpu.VMEM)] * 3,
        scratch_shapes=[
            pltpu.VMEM((half, half), F32),
            pltpu.VMEM((half, half), F32),
            pltpu.VMEM((half, half), F32),
            pltpu.VMEM((half, half), F32),
            pltpu.VMEM((n, half), F32),
            pltpu.VMEM((n, half), F32),
            pltpu.VMEM((2, 2, n, half), F32),
            pltpu.VMEM((len(stages) + 1, 2 * n, 2 * n), F32),
            pltpu.VMEM((slots, 2 * n // members, 2 * n), F32),
            pltpu.VMEM((2 * n, 2 * n), F32),
            dma((1,)), dma((1,)), dma((peers,)), dma((peers,)), dma((2,)), dma((2,)),
            dma((2, 2)), dma((2, 2)), dma((slots,)), dma((slots,)), dma((peers,)), dma((peers,)),
        ],
        compiler_params=pltpu.CompilerParams(
            vmem_limit_bytes=VMEM_LIMIT, collective_id=1, has_side_effects=True
        ),
        name="interface",
    )(own, move, own_mass, move_mass, loads)


def shards(
    interior_factor, coupling, boundary_stiffness, interior_mass, boundary_mass, dof_map, load_cases
):
    own, move, own_mass, move_mass = substructure(
        interior_factor[0], coupling[0], boundary_stiffness[0], interior_mass, boundary_mass, dof_map
    )
    reduced, reduced_mass, found = interface(
        own, move, own_mass, move_mass, load_cases[0], lax.axis_size("sub"), lax.axis_size("grp")
    )
    return (reduced[None], reduced_mass[None], found[None])


def solution(mesh):
    return jax.shard_map(
        shards,
        mesh=mesh,
        in_specs=(
            P("sub", None, None),
            P("sub", "grp", None),
            P("sub", "grp", None),
            P("sub", None),
            P("sub", "grp"),
            P("sub", None),
            P("sub", None, None),
        ),
        out_specs=(P("sub", None, None), P("sub", None, None), P("sub", None, None)),
        check_vma=False,
    )
```

```python
import functools
import jax
import jax.numpy as jnp
from jax import lax
from jax.experimental import pallas as pl
from jax.experimental.pallas import tpu as pltpu
from jax.sharding import PartitionSpec as P

F32 = jnp.float32
BF16 = jnp.bfloat16
HIGH = lax.Precision.HIGHEST
SMALL = 128
TILE = 256
VMEM_LIMIT = 56 * 2**20
NT = (((1,), (1,)), ((), ()))
NN = (((1,), (0,)), ((), ()))
TN = (((0,), (0,)), ((), ()))


def dot(a, b, dims=NN):
    return lax.dot_general(a, b, dims, preferred_element_type=F32)


def fdot(a, b, dims=NN):
    return lax.dot_general(a, b, dims, precision=HIGH, preferred_element_type=F32)


def split(x):
    hi = x.astype(BF16)
    return hi, (x - hi.astype(F32)).astype(BF16)


def dot3(a, b, dims=NN):
    ah, al = split(a)
    bh, bl = split(b)
    return dot(ah, bh, dims) + (dot(ah, bl, dims) + dot(al, bh, dims))


def iota(shape, dim):
    return lax.broadcasted_iota(jnp.int32, shape, dim)


def invert_diagonal(l_ref, inv, small):
    count = l_ref.shape[0] // SMALL
    rows = iota((SMALL, SMALL), 0)
    cols = iota((SMALL, SMALL), 1)

    def block(j):
        return l_ref[j * SMALL : (j + 1) * SMALL, j * SMALL : (j + 1) * SMALL]

    pair = ((rows >> 1) == (cols >> 1)) & (rows > cols)
    for j in range(count):
        full = block(j).astype(F32)
        diag = jnp.where(rows == cols, full, 0.0)
        down = 1.0 / jnp.sum(diag, axis=1, keepdims=True)
        across = 1.0 / jnp.sum(diag, axis=0, keepdims=True)
        first = jnp.where(rows == cols, down, 0.0)
        small[j] = first - jnp.where(pair, down * full * across, 0.0)

    def level(lev, carry):
        same = (rows >> (lev + 1)) == (cols >> (lev + 1))
        low = ((rows >> lev) & 1) > ((cols >> lev) & 1)
        mask = same & low
        for j in range(count):
            x = small[j]
            off = jnp.where(mask, block(j).astype(F32), 0.0).astype(BF16)
            xh, xl = split(x)
            mid = dot(jnp.concatenate([xh, xl], 1), jnp.concatenate([off, off], 0))
            mh, ml = split(mid)
            wide = dot(jnp.concatenate([mh, ml], 1), jnp.concatenate([xh, xh], 0))
            small[j] = x - (wide + dot(mh, xl))
        return carry

    lax.fori_loop(1, SMALL.bit_length() - 1, level, 0)
    for j in range(count // 2):
        upper, lower = small[2 * j], small[2 * j + 1]
        off = l_ref[(2 * j + 1) * SMALL : (2 * j + 2) * SMALL, 2 * j * SMALL : (2 * j + 1) * SMALL]
        lh, ll = split(lower)
        mid = dot(jnp.concatenate([lh, ll], 1), jnp.concatenate([off, off], 0))
        inv[j, :SMALL, :SMALL] = upper
        inv[j, :SMALL, SMALL:] = jnp.zeros((SMALL, SMALL), F32)
        inv[j, SMALL:, :SMALL] = -dot3(mid, upper)
        inv[j, SMALL:, SMALL:] = lower


def solve_modes(l_ref, c_ref, inv, wh, wl):
    for j in range(l_ref.shape[0] // TILE):
        at = slice(j * TILE, (j + 1) * TILE)
        acc = c_ref[:, at].astype(F32)
        if j:
            before = slice(0, j * TILE)
            acc = acc - (
                dot(wh[:, before], l_ref[at, before], NT)
                + dot(wl[:, before], l_ref[at, before], NT)
            )
        wh[:, at], wl[:, at] = split(dot3(acc, inv[j], NT))


def solve_constraint(l_ref, inv, wh, wl):
    ni = l_ref.shape[0]
    for j in reversed(range(ni // TILE)):
        at = slice(j * TILE, (j + 1) * TILE)
        acc = wh[:, at].astype(F32) + wl[:, at].astype(F32)
        if (j + 1) * TILE < ni:
            after = slice((j + 1) * TILE, ni)
            acc = acc + (dot(wh[:, after], l_ref[after, at]) + dot(wl[:, after], l_ref[after, at]))
        wh[:, at], wl[:, at] = split(-dot3(acc, inv[j]))


def inverse_of(p):
    m = len(p)
    if m == 1:
        return [[1.0 / p[0][0]]]
    if m == 2:
        scale = 1.0 / (p[0][0] * p[1][1] - p[0][1] * p[0][1])
        side = -p[0][1] * scale
        return [[p[1][1] * scale, side], [side, p[0][0] * scale]]
    h = m // 2
    span = range(h)
    ai = inverse_of([row[:h] for row in p[:h]])
    b = [row[h:] for row in p[:h]]
    w = [[sum(ai[i][k] * b[k][j] for k in span) for j in span] for i in span]
    s = [[None] * h for _ in span]
    for i in span:
        for j in range(i, h):
            s[i][j] = s[j][i] = p[h + i][h + j] - sum(b[k][i] * w[k][j] for k in span)
    si = inverse_of(s)
    v = [[sum(w[i][k] * si[k][j] for k in span) for j in span] for i in span]
    top = [[None] * h for _ in span]
    for i in span:
        for j in range(i, h):
            top[i][j] = top[j][i] = ai[i][j] + sum(v[i][k] * w[j][k] for k in span)
    out = [top[i] + [-v[i][j] for j in span] for i in span]
    return out + [[-v[j][i] for j in span] + si[i] for i in span]


def sweep(a, size, pivots=8):
    width = a.shape[1]
    lane = iota(a.shape, 1)
    row_at = iota(a.shape, 0)
    first = lane < size
    local = jnp.where(first, lane, lane - size)
    local_row = local[:1]

    def lanes(rows, k):
        left = rows[:, k : k + 1]
        if width == size:
            return jnp.broadcast_to(left, rows.shape)
        return jnp.where(first[: rows.shape[0]], left, rows[:, size + k : size + k + 1])

    for k in range(0, size, pivots):
        span = range(pivots)
        cols = [lanes(a, k + i) for i in span]
        rows = [a[k + i : k + i + 1, :] for i in span]
        small = [[cols[j][k + i : k + i + 1] for j in span] for i in span]
        small = [[small[min(i, j)][max(i, j)] for j in span] for i in span]
        inv = inverse_of(small)
        fresh = []
        for i in span:
            row = sum(inv[i][j] * rows[j] for j in span)
            for j in span:
                row = jnp.where(local_row == k + j, inv[i][j], row)
            fresh.append(row)
        inside = (local // pivots) == (k // pivots)
        a = jnp.where(inside, 0.0, a)
        for i in span:
            a = a - cols[i] * fresh[i]
        for i in span:
            a = jnp.where(row_at == k + i, fresh[i], a)
    return a


def invert(ref, step):
    n = ref.shape[0]
    for p in range(n // step):
        at = slice(p * step, (p + 1) * step)
        pin = sweep(ref[at, at], step)
        panel = ref[at, :]
        col = ref[:, at]
        inside = (iota((step, n), 1) // step) == p
        row = jnp.where(inside, 0.0, dot3(pin, panel))
        left = (iota((n, step), 0) // step) == p
        colz = jnp.where(left, 0.0, col)
        ref[...] = ref[...] - dot3(colz, row)
        ref[:, at] = -dot3(colz, pin)
        ref[at, :] = row
        ref[at, at] = pin


STEP = 64


def stages_of(size):
    stages, stride = [], 1
    while stride < size:
        radix = 4 if stride * 4 <= size else 2
        stages.append((stride, radix))
        stride *= radix
    return stages


def at_device(sub, grp):
    return dict(device_id=(sub, grp), device_id_type=pl.DeviceIdType.MESH)


def reduction_kernel(
    l_hbm, c_hbm, rows_hbm, weights_hbm, bound_hbm, map_hbm, loads_hbm,
    red_ref, mass_ref, out_ref,
    l_ref, c_ref, weights_ref, bound, map_ref, loads_ref, stiff,
    inv, small, wh, wl, both, move, move_mass, came,
    work, z, sy, near, acc, got, total,
    local, send, recv, part_send, part_recv, fwd_send, fwd_recv,
    dir_send, dir_recv, sum_send, sum_recv, all_send, all_recv,
):
    grp, sub = lax.axis_index("grp"), lax.axis_index("sub")
    members, size = lax.axis_size("grp"), lax.axis_size("sub")
    ahead, back = lax.rem(sub + 1, size), lax.rem(sub + size - 1, size)
    others = [lax.rem(grp + d, members) for d in range(1, members)]
    width = c_ref.shape[0]
    half = map_ref.shape[1]
    n = loads_ref.shape[0]
    stages = stages_of(size)
    mine = pl.ds(pl.multiple_of(grp * width, width), width)
    share = half // members
    part = pl.ds(pl.multiple_of(grp * share, share), share)

    loads_in = []
    for i, (src, dst) in enumerate([
        (l_hbm, l_ref), (c_hbm, c_ref), (rows_hbm, stiff.at[mine]), (bound_hbm, bound.at[grp]),
        (weights_hbm, weights_ref), (map_hbm, map_ref), (loads_hbm, loads_ref),
    ]):
        copy = pltpu.make_async_copy(src, dst, local.at[i])
        copy.start()
        loads_in.append(copy)

    def partner(stride, radix, d):
        digit = lax.rem(lax.div(sub, stride), radix)
        return sub + (lax.rem(digit + d, radix) - digit) * stride

    barrier = pltpu.get_barrier_semaphore()
    greeted = 0
    for other in others:
        pl.semaphore_signal(barrier, inc=1, **at_device(sub, other))
        greeted += 1
    for to in [ahead, back] + [partner(t, r, d) for t, r in stages for d in range(1, r)]:
        pl.semaphore_signal(barrier, inc=1, **at_device(to, grp))
        greeted += 1

    def remote(src, dst, send, recv, to_sub, to_grp):
        copy = pltpu.make_async_remote_copy(
            src_ref=src, dst_ref=dst, send_sem=send, recv_sem=recv, **at_device(to_sub, to_grp)
        )
        copy.start()
        return copy

    def spread(item, ref):
        return [
            remote(ref, ref, send.at[item, d], recv.at[item, d], sub, other)
            for d, other in enumerate(others)
        ]

    def to_back(item, ref):
        return remote(ref.at[part], came.at[item, part], part_send.at[item], part_recv.at[item], back, grp)

    def forward(item):
        return [
            remote(
                came.at[item, part], came.at[item, part],
                fwd_send.at[item, d], fwd_recv.at[item, d], sub, other,
            )
            for d, other in enumerate(others)
        ]

    def finished(copies):
        for copy in copies:
            copy.wait()

    loads_in[0].wait()
    invert_diagonal(l_ref, inv, small)
    pl.semaphore_wait(barrier, greeted)
    finished(loads_in[1:])
    stiff_copies = spread(2, stiff.at[mine])
    bound_copies = spread(3, bound.at[grp])
    solve_modes(l_ref, c_ref, inv, wh, wl)
    both[0, mine, :] = wh[...]
    modes_copies = spread(0, both.at[0, mine])
    finished(stiff_copies + modes_copies)

    q = jnp.where(iota((half, half), 0) == map_ref[...], 1.0, 0.0).astype(F32)
    wo, ws = both[0, :half], both[0, half:]
    shared = stiff[half:, half:] - dot(ws, ws, NT)
    move[0] = fdot(fdot(q, shared), q, NT)
    stiff_move = to_back(0, move.at[0])
    cross = stiff[half:, :half] - dot(ws, wo, NT)
    move[1] = fdot(q, cross)
    cross_move = to_back(1, move.at[1])

    solve_constraint(l_ref, inv, wh, wl)
    both[1, mine, :] = wh[...]
    constraint_copies = spread(1, both.at[1, mine])
    red_ref[...] = stiff[:half, :half] - dot(wo, wo, NT)

    stiff_move.wait()
    forwards = forward(0)
    cross_move.wait()
    cross_forwards = forward(1)
    finished(forwards)
    red_ref[...] = red_ref[...] + came[0]
    work[...] = red_ref[...]
    invert(work, STEP)
    z[...] = fdot(loads_ref[...], work[...])

    def neighbours(v, use):
        return [
            remote(v, near.at[use, 0], dir_send.at[use, 0], dir_recv.at[use, 0], ahead, grp),
            remote(v, near.at[use, 1], dir_send.at[use, 1], dir_recv.at[use, 1], back, grp),
        ]

    def from_neighbours(use):
        return fdot(near[use, 0], move[1]) + fdot(near[use, 1], came[1], NT)

    copies = neighbours(z, 0)
    y = fdot(z[...], red_ref[...])
    rho = fdot(loads_ref[...], z[...], NT)
    finished(cross_forwards + bound_copies + constraint_copies)
    weights = weights_ref[...]
    eye = iota((half, half), 0) == iota((half, half), 1)
    pieces = jnp.concatenate([bound[i] for i in range(members)], axis=1)

    def mass_of(c, b):
        ch, cl = split(c.astype(F32) * weights)
        return dot(ch, c, NT) + dot(cl, c, NT) + jnp.where(eye, b, 0.0)

    mass_shared = mass_of(both[1, half:], pieces[:, half:])
    move_mass[...] = fdot(fdot(q, mass_shared), q, NT)
    finished(copies)
    y = y + from_neighbours(0)
    sy[...] = fdot(y, work[...])
    copies = neighbours(sy, 1)
    mass_move = to_back(2, move_mass)
    y2 = fdot(sy[...], red_ref[...])
    acc[0, :n, :n] = rho
    acc[0, :n, n:] = fdot(z[...], y, NT)
    acc[0, n:, :n] = fdot(y, sy[...], NT)
    mass_ref[...] = mass_of(both[1, :half], pieces[:, :half])
    finished(copies)
    y2 = y2 + from_neighbours(1)
    acc[0, n:, n:] = fdot(sy[...], y2, NT)

    rows = 2 * n // members
    chunk = pl.ds(pl.multiple_of(grp * rows, rows), rows)
    slot = 0
    for i, (stride, radix) in enumerate(stages):
        copies = [
            remote(
                acc.at[i, chunk], got.at[slot + d - 1],
                sum_send.at[slot + d - 1], sum_recv.at[slot + d - 1],
                partner(stride, radix, d), grp,
            )
            for d in range(1, radix)
        ]
        value = acc[i, chunk, :]
        for d, copy in enumerate(copies):
            copy.wait()
            value = value + got[slot + d]
        acc[i + 1, chunk, :] = value
        slot += radix - 1
    last = len(stages)
    total[chunk, :] = acc[last, chunk, :]
    copies = [
        remote(acc.at[last, chunk], total.at[chunk], all_send.at[d], all_recv.at[d], sub, other)
        for d, other in enumerate(others)
    ]
    mass_move.wait()
    mass_forwards = forward(2)
    finished(copies)

    rho, gamma = total[:n, :n], total[:n, n:]
    kappa, delta = total[n:, :n], total[n:, n:]
    both = sweep(jnp.concatenate([gamma, rho], axis=1), n)
    gamma_inv, rho_inv = both[:, :n], both[:, n:]
    c1 = fdot(gamma_inv, rho)
    cross = fdot(gamma, c1)
    rho_next = rho - cross - cross.T + fdot(c1, fdot(kappa, c1), TN)
    beta = fdot(rho_inv, rho_next)
    eye = jnp.where(iota((n, n), 0) == iota((n, n), 1), 1.0, 0.0)
    pb = eye + beta
    mixed = fdot(pb, fdot(kappa, c1), TN)
    gamma2 = fdot(pb, fdot(gamma, pb), TN) - mixed - mixed.T + fdot(c1, fdot(delta, c1), TN)
    c2 = fdot(sweep(gamma2, n), rho_next)
    out_ref[...] = fdot(c1 + fdot(pb, c2), z[...], TN) - fdot(fdot(c1, c2), sy[...], TN)
    finished(mass_forwards)
    mass_ref[...] = mass_ref[...] + came[2]


def shards(
    interior_factor, coupling, boundary_stiffness, interior_mass, boundary_mass, dof_map, load_cases
):
    width, ni = coupling.shape[1:]
    nbound = boundary_stiffness.shape[2]
    half = nbound // 2
    n = load_cases.shape[1]
    size, members = lax.axis_size("sub"), lax.axis_size("grp")
    block = jax.ShapeDtypeStruct((half, half), F32)
    stages = stages_of(size)
    slots = sum(r - 1 for _, r in stages)
    peers = max(members - 1, 1)
    dma = pltpu.SemaphoreType.DMA
    outs = pl.pallas_call(
        reduction_kernel,
        out_shape=[block, block, jax.ShapeDtypeStruct((n, half), F32)],
        in_specs=[pl.BlockSpec(memory_space=pltpu.HBM)] * 7,
        out_specs=[pl.BlockSpec(memory_space=pltpu.VMEM)] * 3,
        scratch_shapes=[
            pltpu.VMEM((ni, ni), BF16),
            pltpu.VMEM((width, ni), BF16),
            pltpu.VMEM((1, ni), F32),
            pltpu.VMEM((members, 1, width), F32),
            pltpu.VMEM((1, half), jnp.int32),
            pltpu.VMEM((n, half), F32),
            pltpu.VMEM((nbound, nbound), F32),
            pltpu.VMEM((ni // TILE, TILE, TILE), F32),
            pltpu.VMEM((ni // SMALL, SMALL, SMALL), F32),
            pltpu.VMEM((width, ni), BF16),
            pltpu.VMEM((width, ni), BF16),
            pltpu.VMEM((2, nbound, ni), BF16),
            pltpu.VMEM((2, half, half), F32),
            pltpu.VMEM((half, half), F32),
            pltpu.VMEM((3, half, half), F32),
            pltpu.VMEM((half, half), F32),
            pltpu.VMEM((n, half), F32),
            pltpu.VMEM((n, half), F32),
            pltpu.VMEM((2, 2, n, half), F32),
            pltpu.VMEM((len(stages) + 1, 2 * n, 2 * n), F32),
            pltpu.VMEM((slots, 2 * n // members, 2 * n), F32),
            pltpu.VMEM((2 * n, 2 * n), F32),
            dma((7,)),
            dma((4, peers)), dma((4, peers)), dma((3,)), dma((3,)), dma((3, peers)), dma((3, peers)),
            dma((2, 2)), dma((2, 2)), dma((slots,)), dma((slots,)), dma((peers,)), dma((peers,)),
        ],
        compiler_params=pltpu.CompilerParams(
            vmem_limit_bytes=VMEM_LIMIT, collective_id=0, has_side_effects=True
        ),
        name="reduction",
    )(
        interior_factor[0], coupling[0], boundary_stiffness[0], interior_mass,
        boundary_mass, dof_map, load_cases[0],
    )
    return tuple(out[None] for out in outs)


def solution(mesh):
    return jax.shard_map(
        shards,
        mesh=mesh,
        in_specs=(
            P("sub", None, None),
            P("sub", "grp", None),
            P("sub", "grp", None),
            P("sub", None),
            P("sub", "grp"),
            P("sub", None),
            P("sub", None, None),
        ),
        out_specs=(P("sub", None, None), P("sub", None, None), P("sub", None, None)),
        check_vma=False,
    )
```

```python
import functools
import jax
import jax.numpy as jnp
from jax import lax
from jax.experimental import pallas as pl
from jax.experimental.pallas import tpu as pltpu
from jax.sharding import PartitionSpec as P

F32 = jnp.float32
BF16 = jnp.bfloat16
HIGH = lax.Precision.HIGHEST
SMALL = 128
TILE = 256
VMEM_LIMIT = 56 * 2**20
NT = (((1,), (1,)), ((), ()))
NN = (((1,), (0,)), ((), ()))
TN = (((0,), (0,)), ((), ()))


def dot(a, b, dims=NN):
    return lax.dot_general(a, b, dims, preferred_element_type=F32)


def fdot(a, b, dims=NN):
    return lax.dot_general(a, b, dims, precision=HIGH, preferred_element_type=F32)


def split(x):
    hi = x.astype(BF16)
    return hi, (x - hi.astype(F32)).astype(BF16)


def dot3(a, b, dims=NN):
    ah, al = split(a)
    bh, bl = split(b)
    return dot(ah, bh, dims) + (dot(ah, bl, dims) + dot(al, bh, dims))


def iota(shape, dim):
    return lax.broadcasted_iota(jnp.int32, shape, dim)


def invert_diagonal(l_ref, inv, small):
    count = l_ref.shape[0] // SMALL
    rows = iota((SMALL, SMALL), 0)
    cols = iota((SMALL, SMALL), 1)

    def block(j):
        return l_ref[j * SMALL : (j + 1) * SMALL, j * SMALL : (j + 1) * SMALL]

    pair = ((rows >> 1) == (cols >> 1)) & (rows > cols)
    for j in range(count):
        full = block(j).astype(F32)
        diag = jnp.where(rows == cols, full, 0.0)
        down = 1.0 / jnp.sum(diag, axis=1, keepdims=True)
        across = 1.0 / jnp.sum(diag, axis=0, keepdims=True)
        first = jnp.where(rows == cols, down, 0.0)
        small[j] = first - jnp.where(pair, down * full * across, 0.0)

    def level(lev, carry):
        same = (rows >> (lev + 1)) == (cols >> (lev + 1))
        low = ((rows >> lev) & 1) > ((cols >> lev) & 1)
        mask = same & low
        for j in range(count):
            x = small[j]
            off = jnp.where(mask, block(j).astype(F32), 0.0).astype(BF16)
            xh, xl = split(x)
            mid = dot(jnp.concatenate([xh, xl], 1), jnp.concatenate([off, off], 0))
            mh, ml = split(mid)
            wide = dot(jnp.concatenate([mh, ml], 1), jnp.concatenate([xh, xh], 0))
            small[j] = x - (wide + dot(mh, xl))
        return carry

    lax.fori_loop(1, SMALL.bit_length() - 1, level, 0)
    for j in range(count // 2):
        upper, lower = small[2 * j], small[2 * j + 1]
        off = l_ref[(2 * j + 1) * SMALL : (2 * j + 2) * SMALL, 2 * j * SMALL : (2 * j + 1) * SMALL]
        lh, ll = split(lower)
        mid = dot(jnp.concatenate([lh, ll], 1), jnp.concatenate([off, off], 0))
        inv[j, :SMALL, :SMALL] = upper
        inv[j, :SMALL, SMALL:] = jnp.zeros((SMALL, SMALL), F32)
        inv[j, SMALL:, :SMALL] = -dot3(mid, upper)
        inv[j, SMALL:, SMALL:] = lower


def solve_modes(l_ref, c_ref, inv, wh, wl):
    for j in range(l_ref.shape[0] // TILE):
        at = slice(j * TILE, (j + 1) * TILE)
        acc = c_ref[:, at].astype(F32)
        if j:
            before = slice(0, j * TILE)
            acc = acc - (
                dot(wh[:, before], l_ref[at, before], NT)
                + dot(wl[:, before], l_ref[at, before], NT)
            )
        wh[:, at], wl[:, at] = split(dot3(acc, inv[j], NT))


def solve_constraint(l_ref, inv, wh, wl):
    ni = l_ref.shape[0]
    for j in reversed(range(ni // TILE)):
        at = slice(j * TILE, (j + 1) * TILE)
        acc = wh[:, at].astype(F32) + wl[:, at].astype(F32)
        if (j + 1) * TILE < ni:
            after = slice((j + 1) * TILE, ni)
            acc = acc + (dot(wh[:, after], l_ref[after, at]) + dot(wl[:, after], l_ref[after, at]))
        wh[:, at], wl[:, at] = split(-dot3(acc, inv[j]))


def inverse_of(p):
    m = len(p)
    if m == 1:
        return [[1.0 / p[0][0]]]
    if m == 2:
        scale = 1.0 / (p[0][0] * p[1][1] - p[0][1] * p[0][1])
        side = -p[0][1] * scale
        return [[p[1][1] * scale, side], [side, p[0][0] * scale]]
    h = m // 2
    span = range(h)
    ai = inverse_of([row[:h] for row in p[:h]])
    b = [row[h:] for row in p[:h]]
    w = [[sum(ai[i][k] * b[k][j] for k in span) for j in span] for i in span]
    s = [[None] * h for _ in span]
    for i in span:
        for j in range(i, h):
            s[i][j] = s[j][i] = p[h + i][h + j] - sum(b[k][i] * w[k][j] for k in span)
    si = inverse_of(s)
    v = [[sum(w[i][k] * si[k][j] for k in span) for j in span] for i in span]
    top = [[None] * h for _ in span]
    for i in span:
        for j in range(i, h):
            top[i][j] = top[j][i] = ai[i][j] + sum(v[i][k] * w[j][k] for k in span)
    out = [top[i] + [-v[i][j] for j in span] for i in span]
    return out + [[-v[j][i] for j in span] + si[i] for i in span]


def sweep(a, size, pivots=8):
    width = a.shape[1]
    lane = iota(a.shape, 1)
    row_at = iota(a.shape, 0)
    first = lane < size
    local = jnp.where(first, lane, lane - size)
    local_row = local[:1]

    def lanes(rows, k):
        left = rows[:, k : k + 1]
        if width == size:
            return jnp.broadcast_to(left, rows.shape)
        return jnp.where(first[: rows.shape[0]], left, rows[:, size + k : size + k + 1])

    for k in range(0, size, pivots):
        span = range(pivots)
        cols = [lanes(a, k + i) for i in span]
        rows = [a[k + i : k + i + 1, :] for i in span]
        small = [[cols[j][k + i : k + i + 1] for j in span] for i in span]
        small = [[small[min(i, j)][max(i, j)] for j in span] for i in span]
        inv = inverse_of(small)
        fresh = []
        for i in span:
            row = sum(inv[i][j] * rows[j] for j in span)
            for j in span:
                row = jnp.where(local_row == k + j, inv[i][j], row)
            fresh.append(row)
        inside = (local // pivots) == (k // pivots)
        a = jnp.where(inside, 0.0, a)
        for i in span:
            a = a - cols[i] * fresh[i]
        for i in span:
            a = jnp.where(row_at == k + i, fresh[i], a)
    return a


def invert(ref, step):
    n = ref.shape[0]
    for p in range(n // step):
        at = slice(p * step, (p + 1) * step)
        pin = sweep(ref[at, at], step)
        panel = ref[at, :]
        col = ref[:, at]
        inside = (iota((step, n), 1) // step) == p
        row = jnp.where(inside, 0.0, dot3(pin, panel))
        left = (iota((n, step), 0) // step) == p
        colz = jnp.where(left, 0.0, col)
        ref[...] = ref[...] - dot3(colz, row)
        ref[:, at] = -dot3(colz, pin)
        ref[at, :] = row
        ref[at, at] = pin


STEP = 64


def stages_of(size):
    stages, stride = [], 1
    while stride < size:
        radix = 4 if stride * 4 <= size else 2
        stages.append((stride, radix))
        stride *= radix
    return stages


def at_device(sub, grp):
    return dict(device_id=(sub, grp), device_id_type=pl.DeviceIdType.MESH)


def reduction_kernel(
    l_hbm, c_hbm, rows_hbm, weights_hbm, bound_hbm, map_hbm, loads_hbm,
    red_ref, mass_ref, out_ref,
    l_ref, c_ref, weights_ref, bound, map_ref, loads_ref, stiff,
    inv, small, wh, wl, both, move, move_mass, came,
    work, z, sy, near, acc, got, total,
    local, send, recv, part_send, part_recv, fwd_send, fwd_recv,
    dir_send, dir_recv, sum_send, sum_recv, all_send, all_recv,
):
    grp, sub = lax.axis_index("grp"), lax.axis_index("sub")
    members, size = lax.axis_size("grp"), lax.axis_size("sub")
    ahead, back = lax.rem(sub + 1, size), lax.rem(sub + size - 1, size)
    others = [lax.rem(grp + d, members) for d in range(1, members)]
    width = c_ref.shape[0]
    half = map_ref.shape[1]
    n = loads_ref.shape[0]
    stages = stages_of(size)
    mine = pl.ds(pl.multiple_of(grp * width, width), width)
    share = half // members
    part = pl.ds(pl.multiple_of(grp * share, share), share)

    loads_in = []
    for i, (src, dst) in enumerate([
        (l_hbm, l_ref), (c_hbm, c_ref), (rows_hbm, stiff.at[mine]), (bound_hbm, bound.at[grp]),
        (weights_hbm, weights_ref), (map_hbm, map_ref), (loads_hbm, loads_ref),
    ]):
        copy = pltpu.make_async_copy(src, dst, local.at[i])
        copy.start()
        loads_in.append(copy)

    def partner(stride, radix, d):
        digit = lax.rem(lax.div(sub, stride), radix)
        return sub + (lax.rem(digit + d, radix) - digit) * stride

    barrier = pltpu.get_barrier_semaphore()
    greeted = 0
    for other in others:
        pl.semaphore_signal(barrier, inc=1, **at_device(sub, other))
        greeted += 1
    for to in [ahead, back] + [partner(t, r, d) for t, r in stages for d in range(1, r)]:
        pl.semaphore_signal(barrier, inc=1, **at_device(to, grp))
        greeted += 1

    def remote(src, dst, send, recv, to_sub, to_grp):
        copy = pltpu.make_async_remote_copy(
            src_ref=src, dst_ref=dst, send_sem=send, recv_sem=recv, **at_device(to_sub, to_grp)
        )
        copy.start()
        return copy

    def spread(item, ref):
        return [
            remote(ref, ref, send.at[item, d], recv.at[item, d], sub, other)
            for d, other in enumerate(others)
        ]

    def to_back(item, ref):
        return remote(ref.at[part], came.at[item, part], part_send.at[item], part_recv.at[item], back, grp)

    def forward(item):
        return [
            remote(
                came.at[item, part], came.at[item, part],
                fwd_send.at[item, d], fwd_recv.at[item, d], sub, other,
            )
            for d, other in enumerate(others)
        ]

    def finished(copies):
        for copy in copies:
            copy.wait()

    loads_in[0].wait()
    invert_diagonal(l_ref, inv, small)
    pl.semaphore_wait(barrier, greeted)
    finished(loads_in[1:])
    stiff_copies = spread(2, stiff.at[mine])
    bound_copies = spread(3, bound.at[grp])
    solve_modes(l_ref, c_ref, inv, wh, wl)
    both[0, mine, :] = wh[...]
    modes_copies = spread(0, both.at[0, mine])
    finished(stiff_copies + modes_copies)

    q = jnp.where(iota((half, half), 0) == map_ref[...], 1.0, 0.0).astype(F32)
    wo, ws = both[0, :half], both[0, half:]
    shared = stiff[half:, half:] - dot(ws, ws, NT)
    move[0] = fdot(fdot(q, shared), q, NT)
    stiff_move = to_back(0, move.at[0])
    cross = stiff[half:, :half] - dot(ws, wo, NT)
    move[1] = fdot(q, cross)
    cross_move = to_back(1, move.at[1])

    solve_constraint(l_ref, inv, wh, wl)
    both[1, mine, :] = wh[...]
    constraint_copies = spread(1, both.at[1, mine])
    red_ref[...] = stiff[:half, :half] - dot(wo, wo, NT)

    stiff_move.wait()
    forwards = forward(0)
    cross_move.wait()
    cross_forwards = forward(1)
    finished(forwards)
    red_ref[...] = red_ref[...] + came[0]
    work[...] = red_ref[...]
    invert(work, STEP)
    z[...] = fdot(loads_ref[...], work[...])

    def neighbours(v, use):
        return [
            remote(v, near.at[use, 0], dir_send.at[use, 0], dir_recv.at[use, 0], ahead, grp),
            remote(v, near.at[use, 1], dir_send.at[use, 1], dir_recv.at[use, 1], back, grp),
        ]

    def from_neighbours(use):
        return fdot(near[use, 0], move[1]) + fdot(near[use, 1], came[1], NT)

    copies = neighbours(z, 0)
    y = fdot(z[...], red_ref[...])
    rho = fdot(loads_ref[...], z[...], NT)
    finished(cross_forwards + bound_copies + constraint_copies)
    weights = weights_ref[...]
    eye = iota((half, half), 0) == iota((half, half), 1)
    pieces = jnp.concatenate([bound[i] for i in range(members)], axis=1)

    def mass_of(c, b):
        ch, cl = split(c.astype(F32) * weights)
        return dot(ch, c, NT) + dot(cl, c, NT) + jnp.where(eye, b, 0.0)

    mass_shared = mass_of(both[1, half:], pieces[:, half:])
    move_mass[...] = fdot(fdot(q, mass_shared), q, NT)
    finished(copies)
    y = y + from_neighbours(0)
    sy[...] = fdot(y, work[...])
    copies = neighbours(sy, 1)
    mass_move = to_back(2, move_mass)
    y2 = fdot(sy[...], red_ref[...])
    acc[0, :n, :n] = rho
    acc[0, :n, n:] = fdot(z[...], y, NT)
    acc[0, n:, :n] = fdot(y, sy[...], NT)
    mass_ref[...] = mass_of(both[1, :half], pieces[:, :half])
    finished(copies)
    y2 = y2 + from_neighbours(1)
    acc[0, n:, n:] = fdot(sy[...], y2, NT)

    rows = 2 * n // members
    chunk = pl.ds(pl.multiple_of(grp * rows, rows), rows)
    slot = 0
    for i, (stride, radix) in enumerate(stages):
        copies = [
            remote(
                acc.at[i, chunk], got.at[slot + d - 1],
                sum_send.at[slot + d - 1], sum_recv.at[slot + d - 1],
                partner(stride, radix, d), grp,
            )
            for d in range(1, radix)
        ]
        value = acc[i, chunk, :]
        for d, copy in enumerate(copies):
            copy.wait()
            value = value + got[slot + d]
        acc[i + 1, chunk, :] = value
        slot += radix - 1
    last = len(stages)
    total[chunk, :] = acc[last, chunk, :]
    copies = [
        remote(acc.at[last, chunk], total.at[chunk], all_send.at[d], all_recv.at[d], sub, other)
        for d, other in enumerate(others)
    ]
    mass_move.wait()
    mass_forwards = forward(2)
    finished(copies)

    rho, gamma = total[:n, :n], total[:n, n:]
    kappa, delta = total[n:, :n], total[n:, n:]
    both = sweep(jnp.concatenate([gamma, rho], axis=1), n)
    gamma_inv, rho_inv = both[:, :n], both[:, n:]
    c1 = fdot(gamma_inv, rho)
    cross = fdot(gamma, c1)
    rho_next = rho - cross - cross.T + fdot(c1, fdot(kappa, c1), TN)
    beta = fdot(rho_inv, rho_next)
    eye = jnp.where(iota((n, n), 0) == iota((n, n), 1), 1.0, 0.0)
    pb = eye + beta
    mixed = fdot(pb, fdot(kappa, c1), TN)
    gamma2 = fdot(pb, fdot(gamma, pb), TN) - mixed - mixed.T + fdot(c1, fdot(delta, c1), TN)
    c2 = fdot(sweep(gamma2, n), rho_next)
    out_ref[...] = fdot(c1 + fdot(pb, c2), z[...], TN) - fdot(fdot(c1, c2), sy[...], TN)
    finished(mass_forwards)
    mass_ref[...] = mass_ref[...] + came[2]


def written_kernel(*refs):
    count = len(refs) // 2
    sems = refs[-1]
    copies = [pltpu.make_async_copy(refs[i], refs[count + i], sems.at[i]) for i in range(count)]
    for copy in copies:
        copy.start()
    for copy in copies:
        copy.wait()


def written(arrays):
    return pl.pallas_call(
        written_kernel,
        out_shape=[jax.ShapeDtypeStruct(a.shape, a.dtype) for a in arrays],
        in_specs=[pl.BlockSpec(memory_space=pltpu.HBM)] * len(arrays),
        out_specs=[pl.BlockSpec(memory_space=pltpu.HBM)] * len(arrays),
        scratch_shapes=[pltpu.SemaphoreType.DMA((len(arrays),))],
        name="written",
    )(*arrays)


def shards(
    interior_factor, coupling, boundary_stiffness, interior_mass, boundary_mass, dof_map, load_cases
):
    width, ni = coupling.shape[1:]
    nbound = boundary_stiffness.shape[2]
    half = nbound // 2
    n = load_cases.shape[1]
    size, members = lax.axis_size("sub"), lax.axis_size("grp")
    block = jax.ShapeDtypeStruct((half, half), F32)
    stages = stages_of(size)
    slots = sum(r - 1 for _, r in stages)
    peers = max(members - 1, 1)
    dma = pltpu.SemaphoreType.DMA
    outs = pl.pallas_call(
        reduction_kernel,
        out_shape=[block, block, jax.ShapeDtypeStruct((n, half), F32)],
        in_specs=[pl.BlockSpec(memory_space=pltpu.HBM)] * 7,
        out_specs=[pl.BlockSpec(memory_space=pltpu.VMEM)] * 3,
        scratch_shapes=[
            pltpu.VMEM((ni, ni), BF16),
            pltpu.VMEM((width, ni), BF16),
            pltpu.VMEM((1, ni), F32),
            pltpu.VMEM((members, 1, width), F32),
            pltpu.VMEM((1, half), jnp.int32),
            pltpu.VMEM((n, half), F32),
            pltpu.VMEM((nbound, nbound), F32),
            pltpu.VMEM((ni // TILE, TILE, TILE), F32),
            pltpu.VMEM((ni // SMALL, SMALL, SMALL), F32),
            pltpu.VMEM((width, ni), BF16),
            pltpu.VMEM((width, ni), BF16),
            pltpu.VMEM((2, nbound, ni), BF16),
            pltpu.VMEM((2, half, half), F32),
            pltpu.VMEM((half, half), F32),
            pltpu.VMEM((3, half, half), F32),
            pltpu.VMEM((half, half), F32),
            pltpu.VMEM((n, half), F32),
            pltpu.VMEM((n, half), F32),
            pltpu.VMEM((2, 2, n, half), F32),
            pltpu.VMEM((len(stages) + 1, 2 * n, 2 * n), F32),
            pltpu.VMEM((slots, 2 * n // members, 2 * n), F32),
            pltpu.VMEM((2 * n, 2 * n), F32),
            dma((7,)),
            dma((4, peers)), dma((4, peers)), dma((3,)), dma((3,)), dma((3, peers)), dma((3, peers)),
            dma((2, 2)), dma((2, 2)), dma((slots,)), dma((slots,)), dma((peers,)), dma((peers,)),
        ],
        compiler_params=pltpu.CompilerParams(
            vmem_limit_bytes=VMEM_LIMIT, collective_id=0, has_side_effects=True
        ),
        name="reduction",
    )(
        interior_factor[0], coupling[0], boundary_stiffness[0], interior_mass,
        boundary_mass, dof_map, load_cases[0],
    )
    return tuple(out[None] for out in written(outs))


def solution(mesh):
    return jax.shard_map(
        shards,
        mesh=mesh,
        in_specs=(
            P("sub", None, None),
            P("sub", "grp", None),
            P("sub", "grp", None),
            P("sub", None),
            P("sub", "grp"),
            P("sub", None),
            P("sub", None, None),
        ),
        out_specs=(P("sub", None, None), P("sub", None, None), P("sub", None, None)),
        check_vma=False,
    )
```
